32 devices in a mesh: fsdp: 4 (over z), context: 2 (over y), tensor: 4 (over x, core).
Axes of the slice: x: 2, y: 2, z: 4, core: 2. Of those that a mesh axis runs over, the one named last changes fastest.
Arguments:
- inputs: float32 [4, 512, 1024], P('fsdp', 'context'), may hold values from -6 to 6
- block_len: int32 [4, 2], P('fsdp'), may hold values from 1 to 256, as said below
- leading_norm_gain: float32 [1024], replicated, may hold values from 0.1 to 1.9
- leading_norm_bias: float32 [1024], replicated, may hold values from -2 to 2
- qkv_weight: bfloat16 [1024, 3, 1024], P('fsdp', None, 'tensor'), may hold values from -1 to 1
- qv_bias: float32 [2, 1024], P(None, 'tensor'), may hold values from -3 to 3
- out_weight: bfloat16 [1024, 1024], P('fsdp', 'tensor'), may hold values from -4 to 4
- out_bias: float32 [1024], replicated, may hold values from -2 to 2
- middle_norm_gain: float32 [1024], replicated, may hold values from 0.1 to 1.9
- middle_norm_bias: float32 [1024], replicated, may hold values from -2 to 2
- up_weight: bfloat16 [1024, 4096], P('fsdp', 'tensor'), may hold values from -0.1875 to 0.1875
- up_bias: float32 [4096], P('tensor'), may hold values from -3 to 3
- down_weight: bfloat16 [1024, 4096], P('fsdp', 'tensor'), may hold values from -0.09375 to 0.09375
- down_bias: float32 [1024], replicated, may hold values from -2 to 2
- cotangent: float32 [4, 512, 1024], P('fsdp', 'context'), may hold values from -6 to 6
Outputs:
- outputs: float32 [4, 512, 1024], P('fsdp', 'context')
- grad_inputs: float32 [4, 512, 1024], P('fsdp', 'context')
- grad_pre_gain: float32 [1024], replicated
- grad_pre_shift: float32 [1024], replicated
- grad_qkv_weight: float32 [1024, 3, 1024], P('fsdp', None, 'tensor')
- grad_qv_bias: float32 [2, 1024], P(None, 'tensor')
- grad_out_weight: float32 [1024, 1024], P('fsdp', 'tensor')
- grad_out_bias: float32 [1024], replicated
- grad_mid_gain: float32 [1024], replicated
- grad_mid_shift: float32 [1024], replicated
- grad_up_weight: float32 [1024, 4096], P('fsdp', 'tensor')
- grad_up_bias: float32 [4096], P('tensor')
- grad_down_weight: float32 [1024, 4096], P('fsdp', 'tensor')
- grad_down_bias: float32 [1024], replicated
The draws below stay inside these ranges and needn't reach their ends.
Inputs may be any that keep to these rules, and one draw needn't show every extreme that they name: `block_len`: the live tokens of the 2 blocks of an image add up to 384, and one block of every image holds exactly 256.
All inputs are finite; a program needn't handle non-finite values.
Results may differ from the reference program's by a relative error of at most 0.02.
Values may be sent and summed in bfloat16 or wider, within the bound.
A program may use at most 128 MiB of HBM per device.

```python
import math
import jax
import jax.numpy as jnp
from jax import lax

D = 1024
HEADS = 16
HD = 64
FF = 4096
CAP = 256
SEQ = 384
IMAGES = 4
ROWS = 512
N_CONTEXT = 2


def draw_qkv_weight(key, part):
    base = jax.random.normal(key, (D, 3, D), jnp.float32) * D ** (-0.5)
    return jnp.clip(base, -1.0, 1.0).astype(jnp.bfloat16)


def draw_block_len(key, part):
    full_key = jax.random.fold_in(key, 21)
    weight_key = jax.random.fold_in(key, 22)
    others = N_CONTEXT - 1
    shortfall = N_CONTEXT * CAP - SEQ
    full_block = jax.random.randint(full_key, (IMAGES, 1), 0, N_CONTEXT, dtype=jnp.int32)
    shares = jax.random.randint(weight_key, (IMAGES, others), 1, 4, dtype=jnp.int32)
    share_total = jnp.sum(shares, axis=1, keepdims=True)
    deficit = shortfall * shares // share_total
    leftover = shortfall - jnp.sum(deficit, axis=1, keepdims=True)
    order = jnp.arange(others, dtype=jnp.int32)[None, :]
    deficit = deficit + (order < leftover).astype(jnp.int32)
    blocks = jnp.arange(N_CONTEXT, dtype=jnp.int32)[None, :]
    other_index = blocks - (blocks > full_block).astype(jnp.int32)
    other_index = jnp.clip(other_index, 0, others - 1)
    picked = jnp.take_along_axis(deficit, other_index, axis=1)
    picked = jnp.where(blocks == full_block, 0, picked)
    return (CAP - picked).astype(jnp.int32)


def block_scale(rng, extent, pieces, low, top_value):
    def one(dim, blocks):
        heights = jax.random.uniform(jax.random.fold_in(jax.random.fold_in(rng, 6), dim), (blocks,), jnp.float32, low / len(pieces), top_value / len(pieces))
        return jnp.repeat(jnp.exp(heights), extent[dim] // blocks).reshape((-1,) + (1,) * (len(extent) - dim - 1))

    factor_of = one(*pieces[0])
    for cut in pieces[1:]:
        factor_of = factor_of * one(*cut)
    return factor_of


def noise(key, shape, scale, reach, pieces=(), kind=jnp.bfloat16):
    loudness = block_scale(key, shape, pieces, -0.22, 0.18) if pieces else 1.0
    drawn = jax.random.normal(key, shape, jnp.float32) * scale * loudness
    return jnp.minimum(jnp.maximum(drawn, -reach), reach).astype(kind)


def setup_inputs(seed: int = 0) -> dict:
    streams_of = jax.random.split(jax.random.key(seed), 16)
    return {
        "inputs": noise(streams_of[0], (IMAGES, ROWS, D), 1.0, 6.0, ((0, 4), (1, 2)), jnp.float32),
        "block_len": draw_block_len(jax.random.fold_in(streams_of[15], 71), 0),
        "leading_norm_gain": jnp.clip(1.0 + 0.18 * jax.random.normal(streams_of[2], (D,), jnp.float32), 0.1, 1.9),
        "leading_norm_bias": noise(streams_of[3], (D,), 0.3, 2.0, (), jnp.float32),
        "qkv_weight": draw_qkv_weight(jax.random.fold_in(streams_of[15], 71), 0),
        "qv_bias": noise(streams_of[5], (2, D), 0.5, 3.0, ((1, 4),), jnp.float32),
        "out_weight": noise(streams_of[6], (D, D), (max(1, D // SEQ)) ** -0.5, 4.0, ((0, 4), (1, 4))),
        "out_bias": noise(streams_of[7], (D,), 0.3, 2.0, (), jnp.float32),
        "middle_norm_gain": jnp.clip(1.0 + 0.18 * jax.random.normal(streams_of[8], (D,), jnp.float32), 0.1, 1.9),
        "middle_norm_bias": noise(streams_of[9], (D,), 0.3, 2.0, (), jnp.float32),
        "up_weight": noise(streams_of[10], (D, FF), D ** -0.5, 0.1875, ((0, 4), (1, 4))),
        "up_bias": noise(streams_of[11], (FF,), 0.5, 3.0, ((0, 4),), jnp.float32),
        "down_weight": noise(streams_of[12], (D, FF), FF ** -0.5, 0.09375, ((0, 4), (1, 4))),
        "down_bias": noise(streams_of[13], (D,), 0.3, 2.0, (), jnp.float32),
        "cotangent": noise(streams_of[14], (IMAGES, ROWS, D), 1.0, 6.0, ((0, 4), (1, 2)), jnp.float32),
    }


EPS = 1e-06
SQRT_HALF = 0.7071067811865476
INV_ROOT_TAU = 0.3989422804014327
NEG_BIG = -1e+30

def layer_norm_forward(rows, norm_gain, norm_bias):
    centered_rows = rows - lax.optimization_barrier(jnp.mean(rows, axis=-1, keepdims=True))
    inverse_deviation = lax.rsqrt(lax.optimization_barrier(jnp.mean(centered_rows * centered_rows, axis=-1, keepdims=True)) + EPS)
    normalized_rows = centered_rows * inverse_deviation
    return (normalized_rows * norm_gain + norm_bias, normalized_rows, inverse_deviation)

def layer_norm_backward(output_gradient, normalized_rows, inverse_deviation, norm_gain):
    scaled_rows = output_gradient * norm_gain
    return inverse_deviation * (scaled_rows - lax.optimization_barrier(jnp.mean(scaled_rows, axis=-1, keepdims=True)) - normalized_rows * lax.optimization_barrier(jnp.mean(scaled_rows * normalized_rows, axis=-1, keepdims=True)))

def gelu_value(value):
    return 0.5 * value * (1.0 + lax.erf(value * SQRT_HALF))

def gelu_slope(value):
    return 0.5 * (1.0 + lax.erf(value * SQRT_HALF)) + value * INV_ROOT_TAU * jnp.exp(-0.5 * value * value)

def reference(inputs, block_len, leading_norm_gain, leading_norm_bias, qkv_weight, qv_bias, out_weight, out_bias, middle_norm_gain, middle_norm_bias, up_weight, up_bias, down_weight, down_bias, cotangent):
    rows_total = N_CONTEXT * CAP
    score_scale = 1.0 / math.sqrt(HD)
    qkv_flat = qkv_weight.reshape(D, 3 * D)
    positions = jnp.arange(rows_total, dtype=jnp.int32)

    def split_heads(rows):
        return rows.reshape(rows_total, HEADS, HD).transpose(1, 0, 2)

    def join_heads(heads):
        return heads.transpose(1, 0, 2).reshape(rows_total, D)

    def image_pass(totals, item):
        picture_rows, image_cot, lengths = item
        live_keys = positions % CAP < lengths[(positions // CAP).astype(jnp.int32)]
        live = live_keys.astype(jnp.float32)[:, None]
        first_normed, first_normalized, first_inverse_deviation = layer_norm_forward(picture_rows, leading_norm_gain, leading_norm_bias)
        norm1_b = first_normed.astype(jnp.bfloat16)
        projected = jnp.dot(norm1_b, qkv_flat, preferred_element_type=jnp.float32).reshape(rows_total, 3, D)
        queries = (projected[:, 0] + qv_bias[0]).astype(jnp.bfloat16)
        keys = projected[:, 1].astype(jnp.bfloat16)
        values = (projected[:, 2] + qv_bias[1]).astype(jnp.bfloat16)
        query_heads, key_heads, value_heads = (split_heads(queries), split_heads(keys), split_heads(values))

        def head_forward(operands):
            query_head, key_head, value_head = operands
            scores = jnp.dot(query_head, key_head.T, preferred_element_type=jnp.float32) * score_scale
            scores = jnp.where(live_keys[None, :], scores, NEG_BIG)
            peak = lax.optimization_barrier(jnp.max(scores, axis=1, keepdims=True))
            weights = jnp.where(live_keys[None, :], jnp.exp(scores - peak), 0.0)
            total = lax.optimization_barrier(jnp.sum(weights, axis=1, keepdims=True))
            mixed = jnp.dot(weights.astype(jnp.bfloat16), value_head, preferred_element_type=jnp.float32) / total
            return (mixed, peak + jnp.log(total))
        attn_heads, lse = lax.map(head_forward, (query_heads, key_heads, value_heads))
        attn = join_heads(attn_heads)
        attn_b = attn.astype(jnp.bfloat16)
        residual_rows = picture_rows + jnp.dot(attn_b, out_weight.T, preferred_element_type=jnp.float32) + out_bias
        second_normed, second_normalized, second_inverse_deviation = layer_norm_forward(residual_rows, middle_norm_gain, middle_norm_bias)
        norm2_b = second_normed.astype(jnp.bfloat16)
        pre_act = jnp.dot(norm2_b, up_weight, preferred_element_type=jnp.float32) + up_bias
        hidden = gelu_value(pre_act).astype(jnp.bfloat16)
        result = live * (residual_rows + jnp.dot(hidden, down_weight.T, preferred_element_type=jnp.float32) + down_bias)
        result_gradient = live * image_cot
        grad_y_b = result_gradient.astype(jnp.bfloat16)
        down_weight_gradient = jnp.dot(grad_y_b.T, hidden, preferred_element_type=jnp.float32)
        hidden_gradient = jnp.dot(grad_y_b, down_weight, preferred_element_type=jnp.float32) * gelu_slope(pre_act)
        grad_u_b = hidden_gradient.astype(jnp.bfloat16)
        up_weight_gradient = jnp.dot(norm2_b.T, grad_u_b, preferred_element_type=jnp.float32)
        second_norm_gradient = jnp.dot(grad_u_b, up_weight.T, preferred_element_type=jnp.float32)
        residual_gradient = result_gradient + layer_norm_backward(second_norm_gradient, second_normalized, second_inverse_deviation, middle_norm_gain)
        grad_resid_b = residual_gradient.astype(jnp.bfloat16)
        out_weight_gradient = jnp.dot(grad_resid_b.T, attn_b, preferred_element_type=jnp.float32)
        grad_attn = jnp.dot(grad_resid_b, out_weight, preferred_element_type=jnp.float32).astype(jnp.bfloat16)
        delta = lax.optimization_barrier(jnp.sum((grad_attn.astype(jnp.float32) * attn).reshape(rows_total, HEADS, HD), axis=2)).T[:, :, None]
        grad_attn_heads = split_heads(grad_attn)

        def head_backward(operands):
            query_head, key_head, value_head, grad_head, lse_head, delta_head = operands
            scores = jnp.dot(query_head, key_head.T, preferred_element_type=jnp.float32) * score_scale
            probs = jnp.where(live_keys[None, :], jnp.exp(scores - lse_head), 0.0)
            grad_value = jnp.dot(probs.astype(jnp.bfloat16).T, grad_head, preferred_element_type=jnp.float32)
            grad_probs = jnp.dot(grad_head, value_head.T, preferred_element_type=jnp.float32)
            grad_scores = (probs * (grad_probs - delta_head)).astype(jnp.bfloat16)
            grad_query = score_scale * jnp.dot(grad_scores, key_head, preferred_element_type=jnp.float32)
            grad_key = score_scale * jnp.dot(grad_scores.T, query_head, preferred_element_type=jnp.float32)
            return (grad_query, grad_key, grad_value)
        grad_qh, grad_kh, grad_vh = lax.map(head_backward, (query_heads, key_heads, value_heads, grad_attn_heads, lse, delta))
        queries_gradient, grad_keys, values_gradient = (join_heads(grad_qh), join_heads(grad_kh), join_heads(grad_vh))
        grad_p = jnp.stack([queries_gradient, grad_keys, values_gradient], axis=1).astype(jnp.bfloat16).reshape(rows_total, 3 * D)
        query_key_value_weight_gradient = jnp.dot(norm1_b.T, grad_p, preferred_element_type=jnp.float32).reshape(D, 3, D)
        first_norm_gradient = jnp.dot(grad_p, qkv_flat.T, preferred_element_type=jnp.float32)
        input_gradient = residual_gradient + layer_norm_backward(first_norm_gradient, first_normalized, first_inverse_deviation, leading_norm_gain)
        gradient_terms = (lax.optimization_barrier(jnp.sum(first_norm_gradient * first_normalized, axis=0)), lax.optimization_barrier(jnp.sum(first_norm_gradient, axis=0)), query_key_value_weight_gradient, jnp.stack([lax.optimization_barrier(jnp.sum(queries_gradient, axis=0)), lax.optimization_barrier(jnp.sum(values_gradient, axis=0))]), out_weight_gradient, lax.optimization_barrier(jnp.sum(residual_gradient, axis=0)), lax.optimization_barrier(jnp.sum(second_norm_gradient * second_normalized, axis=0)), lax.optimization_barrier(jnp.sum(second_norm_gradient, axis=0)), up_weight_gradient, lax.optimization_barrier(jnp.sum(hidden_gradient, axis=0)), down_weight_gradient, lax.optimization_barrier(jnp.sum(result_gradient, axis=0)))
        totals = tuple((total + term for total, term in zip(totals, gradient_terms)))
        return (totals, (result, input_gradient))
    zeros = (jnp.zeros((D,), jnp.float32), jnp.zeros((D,), jnp.float32), jnp.zeros((D, 3, D), jnp.float32), jnp.zeros((2, D), jnp.float32), jnp.zeros((D, D), jnp.float32), jnp.zeros((D,), jnp.float32), jnp.zeros((D,), jnp.float32), jnp.zeros((D,), jnp.float32), jnp.zeros((D, FF), jnp.float32), jnp.zeros((FF,), jnp.float32), jnp.zeros((D, FF), jnp.float32), jnp.zeros((D,), jnp.float32))
    totals, stacked = lax.scan(image_pass, zeros, (inputs, cotangent, block_len))
    outputs, grad_inputs = stacked
    return (outputs, grad_inputs, totals[0], totals[1], totals[2], totals[3], totals[4], totals[5], totals[6], totals[7], totals[8], totals[9], totals[10], totals[11])
```

```python
import functools
import math

import jax
import jax.numpy as jnp
from jax import lax
from jax.sharding import PartitionSpec as P

HD = 64


EPS = 1e-06
SQRT_HALF = 0.7071067811865476
INV_ROOT_TAU = 0.3989422804014327
NEG_BIG = -1e30
MOST_DIRECT = 16


def layer_norm_forward(rows, norm_gain, norm_bias):
    centered_rows = rows - jnp.mean(rows, axis=-1, keepdims=True)
    inverse_deviation = lax.rsqrt(
        jnp.mean(centered_rows * centered_rows, axis=-1, keepdims=True) + EPS
    )
    normalized_rows = centered_rows * inverse_deviation
    return (normalized_rows * norm_gain + norm_bias, normalized_rows, inverse_deviation)


def layer_norm_backward(output_gradient, normalized_rows, inverse_deviation, norm_gain):
    scaled_rows = output_gradient * norm_gain
    return inverse_deviation * (
        scaled_rows
        - jnp.mean(scaled_rows, axis=-1, keepdims=True)
        - normalized_rows * jnp.mean(scaled_rows * normalized_rows, axis=-1, keepdims=True)
    )


def gelu_value(value):
    return 0.5 * value * (1.0 + lax.erf(value * SQRT_HALF))


def gelu_slope(value):
    return 0.5 * (1.0 + lax.erf(value * SQRT_HALF)) + value * INV_ROOT_TAU * jnp.exp(
        -0.5 * value * value
    )


def rotate(x, axis, count, step):
    return lax.ppermute(x, axis, [(i, (i + step) % count) for i in range(count)])


def take_block(x, index, rows):
    return lax.dynamic_slice_in_dim(x, index * rows, rows, axis=0)


def gather_weight(shard, fsdp_count, context_count):
    if fsdp_count * context_count > MOST_DIRECT:
        return lax.all_gather(shard, "fsdp", axis=0, tiled=True)
    place, position = lax.axis_index("fsdp"), lax.axis_index("context")
    shard_rows, columns = shard.shape
    part_rows = shard_rows // context_count
    own_part = take_block(shard, position, part_rows)
    full = jnp.zeros((fsdp_count * shard_rows, columns), shard.dtype)
    full = lax.dynamic_update_slice_in_dim(full, shard, place * shard_rows, axis=0)
    for step in range(1, fsdp_count):
        arrived = rotate(own_part, "fsdp", fsdp_count, step)
        base = ((place - step) % fsdp_count) * shard_rows
        full = lax.dynamic_update_slice_in_dim(full, arrived, base + position * part_rows, axis=0)
        for turn in range(1, context_count):
            shared = rotate(arrived, "context", context_count, turn)
            owner = (position - turn) % context_count
            full = lax.dynamic_update_slice_in_dim(full, shared, base + owner * part_rows, axis=0)
    return full


def scatter_gradient(rows_left, rows_right, fsdp_count, context_count):
    if fsdp_count * context_count > MOST_DIRECT:
        whole = jnp.dot(rows_left.T, rows_right, preferred_element_type=jnp.float32)
        owned = lax.psum_scatter(
            whole.astype(jnp.bfloat16), "fsdp", scatter_dimension=0, tiled=True
        )
        return lax.psum(owned, "context").astype(jnp.float32)
    place, position = lax.axis_index("fsdp"), lax.axis_index("context")
    tokens, features = rows_left.shape
    columns = rows_right.shape[1]
    shard_rows = features // fsdp_count
    part_rows = shard_rows // context_count
    parted = rows_left.reshape(tokens, fsdp_count, context_count, part_rows)

    def partial(index):
        chosen = lax.dynamic_slice_in_dim(parted, index, 1, axis=2)
        return jnp.dot(
            chosen.reshape(tokens, fsdp_count * part_rows).T,
            rows_right,
            preferred_element_type=jnp.float32,
        )

    arrived = [
        rotate(
            partial((position + turn) % context_count).astype(jnp.bfloat16),
            "context",
            context_count,
            turn,
        )
        for turn in range(1, context_count)
    ]
    total = partial(position)
    for piece in arrived:
        total = total + piece.astype(jnp.float32)
    landed = [
        rotate(
            take_block(total, (place + step) % fsdp_count, part_rows).astype(jnp.bfloat16),
            "fsdp",
            fsdp_count,
            step,
        )
        for step in range(1, fsdp_count)
    ]
    owned = take_block(total, place, part_rows)
    for piece in landed:
        owned = owned + piece.astype(jnp.float32)
    owned = owned.astype(jnp.bfloat16)
    result = jnp.zeros((shard_rows, columns), jnp.float32)
    result = lax.dynamic_update_slice_in_dim(
        result, owned.astype(jnp.float32), position * part_rows, axis=0
    )
    for turn in range(1, context_count):
        shared = rotate(owned, "context", context_count, turn)
        owner = (position - turn) % context_count
        result = lax.dynamic_update_slice_in_dim(
            result, shared.astype(jnp.float32), owner * part_rows, axis=0
        )
    return result


def swap(x, axis, count, bit):
    return lax.ppermute(x, axis, [(i, i ^ bit) for i in range(count)])


def sum_tensor(part, tensor_count):
    if tensor_count != 4:
        return lax.psum(part.astype(jnp.bfloat16), "tensor").astype(jnp.float32)
    core = lax.axis_index("tensor") % 2
    half = part.shape[0] // 2
    kept = take_block(part, core, half)
    sent = take_block(part, 1 - core, half).astype(jnp.bfloat16)
    pair = (kept + swap(sent, "tensor", 4, 1).astype(jnp.float32)).astype(jnp.bfloat16)
    other = swap(pair, "tensor", 4, 2)
    total = (pair.astype(jnp.float32) + other.astype(jnp.float32)).astype(jnp.bfloat16)
    mate = swap(total, "tensor", 4, 1)
    low = jnp.where(core == 0, total, mate)
    high = jnp.where(core == 0, mate, total)
    return jnp.concatenate([low, high], axis=0).astype(jnp.float32)


def sum_small(x, fsdp_count, context_count):
    for axis, count in (("context", context_count), ("fsdp", fsdp_count)):
        if count & (count - 1):
            x = lax.psum(x, axis)
            continue
        bit = 1
        while bit < count:
            x = x + swap(x, axis, count, bit)
            bit *= 2
    return x


def split_heads(rows):
    return rows.reshape(rows.shape[0], -1, HD).transpose(1, 0, 2)


def join_heads(heads):
    return heads.transpose(1, 0, 2).reshape(heads.shape[1], -1)


def local(
    fsdp_count,
    context_count,
    tensor_count,
    inputs,
    block_len,
    leading_norm_gain,
    leading_norm_bias,
    qkv_weight,
    qv_bias,
    out_weight,
    out_bias,
    middle_norm_gain,
    middle_norm_bias,
    up_weight,
    up_bias,
    down_weight,
    down_bias,
    cotangent,
):
    incoming_rows = inputs[0]
    block_rows = incoming_rows.shape[0]
    lengths = block_len[0]
    score_scale = 1.0 / math.sqrt(HD)
    position = lax.axis_index("context")
    slots = jnp.arange(block_rows, dtype=jnp.int32)

    def length_of(owner):
        table = jnp.arange(context_count, dtype=jnp.int32)
        return jnp.sum(jnp.where(table == owner, lengths, 0))

    live = (slots < length_of(position)).astype(jnp.float32)[:, None]
    local_width = qkv_weight.shape[2]
    qkv_full = gather_weight(
        qkv_weight.reshape(qkv_weight.shape[0], 3 * local_width), fsdp_count, context_count
    )
    out_full = gather_weight(out_weight, fsdp_count, context_count)
    up_full = gather_weight(up_weight, fsdp_count, context_count)
    down_full = gather_weight(down_weight, fsdp_count, context_count)

    first_normed, first_normalized, first_inverse_deviation = layer_norm_forward(
        incoming_rows, leading_norm_gain, leading_norm_bias
    )
    norm1_b = first_normed.astype(jnp.bfloat16)
    projected = jnp.dot(norm1_b, qkv_full, preferred_element_type=jnp.float32)
    queries = (projected[:, :local_width] + qv_bias[0]).astype(jnp.bfloat16)
    keys = projected[:, local_width : 2 * local_width].astype(jnp.bfloat16)
    values = (projected[:, 2 * local_width :] + qv_bias[1]).astype(jnp.bfloat16)
    keys_values = jnp.concatenate([keys, values], axis=1)
    pieces = [keys_values] + [
        rotate(keys_values, "context", context_count, turn) for turn in range(1, context_count)
    ]
    owners = [(position - turn) % context_count for turn in range(context_count)]
    live_keys = jnp.concatenate([slots < length_of(owner) for owner in owners])[None, None, :]
    query_heads = split_heads(queries)
    key_heads = jnp.concatenate([split_heads(p[:, :local_width]) for p in pieces], axis=1)
    value_heads = jnp.concatenate([split_heads(p[:, local_width:]) for p in pieces], axis=1)
    scores = (
        jnp.einsum("hqe,hke->hqk", query_heads, key_heads, preferred_element_type=jnp.float32)
        * score_scale
    )
    scores = jnp.where(live_keys, scores, NEG_BIG)
    peak = jnp.max(scores, axis=2, keepdims=True)
    weights = jnp.where(live_keys, jnp.exp(scores - peak), 0.0)
    total = jnp.sum(weights, axis=2, keepdims=True)
    attn_heads = (
        jnp.einsum(
            "hqk,hke->hqe",
            weights.astype(jnp.bfloat16),
            value_heads,
            preferred_element_type=jnp.float32,
        )
        / total
    )
    attn_b = join_heads(attn_heads.astype(jnp.bfloat16))
    attn_part = jnp.dot(attn_b, out_full.T, preferred_element_type=jnp.float32)
    residual_rows = incoming_rows + sum_tensor(attn_part, tensor_count) + out_bias
    second_normed, second_normalized, second_inverse_deviation = layer_norm_forward(
        residual_rows, middle_norm_gain, middle_norm_bias
    )
    norm2_b = second_normed.astype(jnp.bfloat16)
    pre_act = jnp.dot(norm2_b, up_full, preferred_element_type=jnp.float32) + up_bias
    hidden = gelu_value(pre_act).astype(jnp.bfloat16)
    result_gradient = live * cotangent[0]
    grad_y_b = result_gradient.astype(jnp.bfloat16)
    down_owned = scatter_gradient(grad_y_b, hidden, fsdp_count, context_count)
    hidden_gradient = jnp.dot(grad_y_b, down_full, preferred_element_type=jnp.float32) * gelu_slope(
        pre_act
    )
    grad_u_b = hidden_gradient.astype(jnp.bfloat16)
    second_norm_gradient = sum_tensor(
        jnp.dot(grad_u_b, up_full.T, preferred_element_type=jnp.float32), tensor_count
    )
    up_owned = scatter_gradient(norm2_b, grad_u_b, fsdp_count, context_count)
    mlp_part = jnp.dot(hidden, down_full.T, preferred_element_type=jnp.float32)
    result = live * (residual_rows + sum_tensor(mlp_part, tensor_count) + down_bias)
    residual_gradient = result_gradient + layer_norm_backward(
        second_norm_gradient, second_normalized, second_inverse_deviation, middle_norm_gain
    )
    grad_resid_b = residual_gradient.astype(jnp.bfloat16)
    out_owned = scatter_gradient(grad_resid_b, attn_b, fsdp_count, context_count)
    grad_attn = jnp.dot(grad_resid_b, out_full, preferred_element_type=jnp.float32).astype(
        jnp.bfloat16
    )
    grad_attn_heads = split_heads(grad_attn)
    delta = jnp.sum(grad_attn_heads.astype(jnp.float32) * attn_heads, axis=2, keepdims=True)
    probs = weights / total
    grad_probs = jnp.einsum(
        "hqe,hke->hqk", grad_attn_heads, value_heads, preferred_element_type=jnp.float32
    )
    grad_scores = (probs * (grad_probs - delta)).astype(jnp.bfloat16)
    grad_value_heads = jnp.einsum(
        "hqk,hqe->hke",
        probs.astype(jnp.bfloat16),
        grad_attn_heads,
        preferred_element_type=jnp.float32,
    )
    grad_key_heads = score_scale * jnp.einsum(
        "hqk,hqe->hke", grad_scores, query_heads, preferred_element_type=jnp.float32
    )
    grad_query_heads = score_scale * jnp.einsum(
        "hqk,hke->hqe", grad_scores, key_heads, preferred_element_type=jnp.float32
    )
    queries_gradient = join_heads(grad_query_heads)

    def terms(turn):
        rows = slice(turn * block_rows, (turn + 1) * block_rows)
        return jnp.concatenate(
            [join_heads(grad_key_heads[:, rows]), join_heads(grad_value_heads[:, rows])], axis=1
        )

    keys_values_gradient = terms(0)
    for turn in range(1, context_count):
        keys_values_gradient = keys_values_gradient + rotate(
            terms(turn).astype(jnp.bfloat16), "context", context_count, -turn
        ).astype(jnp.float32)
    grad_p = jnp.concatenate([queries_gradient, keys_values_gradient], axis=1).astype(jnp.bfloat16)
    first_norm_gradient = sum_tensor(
        jnp.dot(grad_p, qkv_full.T, preferred_element_type=jnp.float32), tensor_count
    )
    qkv_owned = scatter_gradient(norm1_b, grad_p, fsdp_count, context_count).reshape(
        qkv_weight.shape
    )
    input_gradient = residual_gradient + layer_norm_backward(
        first_norm_gradient, first_normalized, first_inverse_deviation, leading_norm_gain
    )
    early = sum_small(
        jnp.concatenate(
            [
                jnp.sum(residual_gradient, axis=0),
                jnp.sum(second_norm_gradient * second_normalized, axis=0),
                jnp.sum(second_norm_gradient, axis=0),
                jnp.sum(result_gradient, axis=0),
                jnp.sum(hidden_gradient, axis=0),
            ]
        ),
        fsdp_count,
        context_count,
    )
    late = sum_small(
        jnp.concatenate(
            [
                jnp.sum(first_norm_gradient * first_normalized, axis=0),
                jnp.sum(first_norm_gradient, axis=0),
                jnp.sum(queries_gradient, axis=0),
                jnp.sum(keys_values_gradient[:, local_width:], axis=0),
            ]
        ),
        fsdp_count,
        context_count,
    )
    width = incoming_rows.shape[1]
    return (
        result[None],
        input_gradient[None],
        late[:width],
        late[width : 2 * width],
        qkv_owned,
        late[2 * width :].reshape(2, local_width),
        out_owned,
        early[:width],
        early[width : 2 * width],
        early[2 * width : 3 * width],
        up_owned,
        early[4 * width :],
        down_owned,
        early[3 * width : 4 * width],
    )


def solution(mesh):
    in_specs = (
        P("fsdp", "context", None),
        P("fsdp", None),
        P(),
        P(),
        P("fsdp", None, "tensor"),
        P(None, "tensor"),
        P("fsdp", "tensor"),
        P(),
        P(),
        P(),
        P("fsdp", "tensor"),
        P("tensor"),
        P("fsdp", "tensor"),
        P(),
        P("fsdp", "context", None),
    )
    out_specs = (
        P("fsdp", "context", None),
        P("fsdp", "context", None),
        P(),
        P(),
        P("fsdp", None, "tensor"),
        P(None, "tensor"),
        P("fsdp", "tensor"),
        P(),
        P(),
        P(),
        P("fsdp", "tensor"),
        P("tensor"),
        P("fsdp", "tensor"),
        P(),
    )
    return jax.shard_map(functools.partial(local, mesh.shape["fsdp"], mesh.shape["context"], mesh.shape["tensor"]), mesh=mesh, in_specs=in_specs, out_specs=out_specs, check_vma=False)
```

```python
import functools
import math

import jax
import jax.numpy as jnp
from jax import lax
from jax.experimental import pallas as pl
from jax.experimental.pallas import tpu as pltpu
from jax.sharding import PartitionSpec as P

HD = 64


EPS = 1e-06
SQRT_HALF = 0.7071067811865476
INV_ROOT_TAU = 0.3989422804014327
NEG_BIG = -1e30


def layer_norm_forward(rows, norm_gain, norm_bias):
    centered_rows = rows - jnp.mean(rows, axis=-1, keepdims=True)
    inverse_deviation = lax.rsqrt(
        jnp.mean(centered_rows * centered_rows, axis=-1, keepdims=True) + EPS
    )
    normalized_rows = centered_rows * inverse_deviation
    return (normalized_rows * norm_gain + norm_bias, normalized_rows, inverse_deviation)


def layer_norm_backward(output_gradient, normalized_rows, inverse_deviation, norm_gain):
    scaled_rows = output_gradient * norm_gain
    return inverse_deviation * (
        scaled_rows
        - jnp.mean(scaled_rows, axis=-1, keepdims=True)
        - normalized_rows * jnp.mean(scaled_rows * normalized_rows, axis=-1, keepdims=True)
    )


def gelu_value(value):
    return 0.5 * value * (1.0 + lax.erf(value * SQRT_HALF))


def gelu_slope(value):
    return 0.5 * (1.0 + lax.erf(value * SQRT_HALF)) + value * INV_ROOT_TAU * jnp.exp(
        -0.5 * value * value
    )


def rotate(x, axis, count, step):
    return lax.ppermute(x, axis, [(i, (i + step) % count) for i in range(count)])


MESH = pl.DeviceIdType.MESH
WHOLE = pl.BlockSpec(memory_space=pltpu.VMEM)


def remote(source, target, send, receive, where):
    copy = pltpu.make_async_remote_copy(
        src_ref=source,
        dst_ref=target,
        send_sem=send,
        recv_sem=receive,
        device_id=where,
        device_id_type=MESH,
    )
    return copy


def rows_of(index, rows):
    return pl.ds(pl.multiple_of(index * rows, rows), rows)


def greet(partners):
    barrier = pltpu.get_barrier_semaphore()
    for partner in partners:
        pl.semaphore_signal(barrier, inc=1, device_id=partner, device_id_type=MESH)
    pl.semaphore_wait(barrier, len(partners))


def gather_kernel(count, fsdp_count, *refs):
    shards, fulls = refs[:count], refs[count : 2 * count]
    up_send, down_send, line_recv, side_send, side_recv = refs[2 * count :]
    place, position = lax.axis_index("fsdp"), lax.axis_index("context")
    mate = {"context": 1 - position}
    above, below = {"fsdp": place + 1}, {"fsdp": place - 1}
    has_above, has_below = place < fsdp_count - 1, place > 0
    greet(
        [mate] + [{"fsdp": lax.rem(place + step, fsdp_count)} for step in range(1, fsdp_count)]
    )

    def part(w, owner):
        shard_rows = shards[w].shape[0]
        half = shard_rows // 2
        start = pl.multiple_of(owner * shard_rows + position * half, half)
        return fulls[w].at[pl.ds(start, half)]

    def far_part(w, owner):
        shard_rows = shards[w].shape[0]
        half = shard_rows // 2
        start = pl.multiple_of(owner * shard_rows + (1 - position) * half, half)
        return fulls[w].at[pl.ds(start, half)]

    def own(w):
        return shards[w].at[rows_of(position, shards[w].shape[0] // 2)]

    def upward(w, owner, source):
        return remote(source, part(w, owner), up_send.at[w, owner], line_recv.at[w, owner], above)

    def downward(w, owner, source):
        return remote(
            source, part(w, owner), down_send.at[w, owner], line_recv.at[w, owner], below
        )

    def sideways(w, owner):
        block = part(w, owner)
        return remote(block, block, side_send.at[w, owner], side_recv.at[w, owner], mate)

    for w in range(count):

        @pl.when(has_above)
        def _():
            upward(w, place, own(w)).start()

        @pl.when(has_below)
        def _():
            downward(w, place, own(w)).start()

    for w in range(count):
        fulls[w][rows_of(place, shards[w].shape[0]), :] = shards[w][...]
    for w in range(count):
        for distance in range(1, fsdp_count):
            low, high = place - distance, place + distance

            @pl.when(low >= 0)
            def _():
                block = part(w, low)
                upward(w, low, block).wait_recv()

                @pl.when(has_above)
                def _():
                    upward(w, low, block).start()

                sideways(w, low).start()

            @pl.when(high < fsdp_count)
            def _():
                block = part(w, high)
                downward(w, high, block).wait_recv()

                @pl.when(has_below)
                def _():
                    downward(w, high, block).start()

                sideways(w, high).start()

    for w in range(count):

        @pl.when(has_above)
        def _():
            upward(w, place, own(w)).wait_send()

        @pl.when(has_below)
        def _():
            downward(w, place, own(w)).wait_send()

        for distance in range(1, fsdp_count):
            low, high = place - distance, place + distance

            @pl.when(low >= 0)
            def _():
                block = part(w, low)

                @pl.when(has_above)
                def _():
                    upward(w, low, block).wait_send()

                sideways(w, low).wait_send()
                other = far_part(w, low)
                remote(
                    other, other, side_send.at[w, low], side_recv.at[w, low], mate
                ).wait_recv()

            @pl.when(high < fsdp_count)
            def _():
                block = part(w, high)

                @pl.when(has_below)
                def _():
                    downward(w, high, block).wait_send()

                sideways(w, high).wait_send()
                other = far_part(w, high)
                remote(
                    other, other, side_send.at[w, high], side_recv.at[w, high], mate
                ).wait_recv()


def gather_weights(shards, fsdp_count, context_count):
    if not direct(fsdp_count, context_count):
        return [lax.all_gather(shard, "fsdp", axis=0, tiled=True) for shard in shards]
    count = len(shards)
    sems = pltpu.SemaphoreType.DMA((count, fsdp_count))
    return pl.pallas_call(
        functools.partial(gather_kernel, count, fsdp_count),
        out_shape=[
            jax.ShapeDtypeStruct((fsdp_count * x.shape[0], x.shape[1]), x.dtype) for x in shards
        ],
        in_specs=[WHOLE] * count,
        out_specs=[WHOLE] * count,
        scratch_shapes=[sems] * 5,
        compiler_params=pltpu.CompilerParams(collective_id=0, has_side_effects=True),
        name="gather_weights",
    )(*shards)


def direct(fsdp_count, context_count):
    return context_count == 2 and fsdp_count in (2, 4)


def scatter_kernel(count, fsdp_count, *refs):
    lefts, rights = refs[:count], refs[count : 2 * count]
    small = refs[2 * count]
    outs = refs[2 * count + 1 : 3 * count + 1]
    small_out = refs[3 * count + 1]
    rest = refs[3 * count + 2 :]
    side_out, side_in, line_out, line_in, last_out, last_in = (
        rest[i * count : (i + 1) * count] for i in range(6)
    )
    (
        small_sum,
        small_in,
        side_send,
        side_recv,
        line_send,
        line_recv,
        last_send,
        last_recv,
        small_send,
        small_recv,
    ) = rest[6 * count :]
    place, position = lax.axis_index("fsdp"), lax.axis_index("context")
    other = 1 - position
    mate = {"context": other}
    features = lefts[0].shape[1]
    shard_rows = features // fsdp_count
    half = shard_rows // 2
    greet(
        [mate] + [{"fsdp": lax.rem(place + step, fsdp_count)} for step in range(1, fsdp_count)]
    )

    def product(w, step, side):
        owner = lax.rem(place + step, fsdp_count)
        start = pl.multiple_of(owner * shard_rows + side * half, half)
        return lax.dot_general(
            lefts[w][:, pl.ds(start, half)],
            rights[w][...],
            (((0,), (0,)), ((), ())),
            preferred_element_type=jnp.float32,
        )

    hops = [mate]
    bit = 1
    while bit < fsdp_count:
        hops.append({"fsdp": jnp.bitwise_xor(place, bit)})
        bit *= 2
    small_copies = []

    def small_hop(hop):
        source = small if hop == 0 else small_sum.at[hop - 1]
        copy = remote(
            source, small_in.at[hop], small_send.at[hop], small_recv.at[hop], hops[hop]
        )
        copy.start()
        small_copies.append(copy)

    def small_add(hop):
        small_copies[hop].wait_recv()
        before = small[...] if hop == 0 else small_sum[hop - 1]
        after = before + small_in[hop]
        if hop + 1 == len(hops):
            small_out[...] = after
        else:
            small_sum[hop] = after

    small_hop(0)
    sends = []
    side_copies = {}
    order = [step % fsdp_count for step in range(1, fsdp_count + 1)]
    for w in range(count):
        for step in order:
            side_out[w][step] = product(w, step, other).astype(jnp.bfloat16)
            copy = remote(
                side_out[w].at[step],
                side_in[w].at[step],
                side_send.at[w, step],
                side_recv.at[w, step],
                mate,
            )
            copy.start()
            side_copies[w, step] = copy
            sends.append(copy)
        if w < len(hops):
            small_add(w)
            if w + 1 < len(hops):
                small_hop(w + 1)
    line_copies = {}
    last_copies = []

    def settle(w):
        total = outs[w][rows_of(position, half), :]
        for step in range(1, fsdp_count):
            line_copies[w, step].wait_recv()
            total = total + line_in[w][step - 1].astype(jnp.float32)
        rounded = total.astype(jnp.bfloat16)
        last_out[w][...] = rounded
        copy = remote(last_out[w], last_in[w], last_send.at[w], last_recv.at[w], mate)
        copy.start()
        last_copies.append(copy)
        sends.append(copy)
        outs[w][rows_of(position, half), :] = rounded.astype(jnp.float32)

    for w in range(count):
        for step in order:
            mine = product(w, step, position)
            side_copies[w, step].wait_recv()
            mine = mine + side_in[w][step].astype(jnp.float32)
            if step == 0:
                outs[w][rows_of(position, half), :] = mine
                continue
            line_out[w][step - 1] = mine.astype(jnp.bfloat16)
            copy = remote(
                line_out[w].at[step - 1],
                line_in[w].at[step - 1],
                line_send.at[w, step - 1],
                line_recv.at[w, step - 1],
                {"fsdp": lax.rem(place + step, fsdp_count)},
            )
            copy.start()
            line_copies[w, step] = copy
            sends.append(copy)
        if w > 0:
            settle(w - 1)
    settle(count - 1)
    for w in range(count):
        last_copies[w].wait_recv()
        outs[w][rows_of(other, half), :] = last_in[w][...].astype(jnp.float32)
    for copy in small_copies + sends:
        copy.wait_send()


def scatter_gradients(pairs, small, fsdp_count, context_count):
    if not direct(fsdp_count, context_count):
        owned = []
        for left, right in pairs:
            whole = jnp.dot(left.T, right, preferred_element_type=jnp.float32)
            part = lax.psum_scatter(
                whole.astype(jnp.bfloat16), "fsdp", scatter_dimension=0, tiled=True
            )
            owned.append(lax.psum(part, "context").astype(jnp.float32))
        return owned, lax.psum(small, ("fsdp", "context"))
    count = len(pairs)
    lefts, rights = [p[0] for p in pairs], [p[1] for p in pairs]
    length = small.shape[0]
    padded = -(-length // 1024) * 1024
    small = jnp.pad(small, (0, padded - length)).reshape(padded // 128, 128)
    shard_rows = lefts[0].shape[1] // fsdp_count
    half = shard_rows // 2
    widths = [x.shape[1] for x in rights]

    def buffers(*lead):
        return [pltpu.VMEM((*lead, half, width), jnp.bfloat16) for width in widths]

    hops = 1 + (fsdp_count - 1).bit_length()
    dma = pltpu.SemaphoreType.DMA
    result = pl.pallas_call(
        functools.partial(scatter_kernel, count, fsdp_count),
        out_shape=[jax.ShapeDtypeStruct((shard_rows, width), jnp.float32) for width in widths]
        + [jax.ShapeDtypeStruct(small.shape, jnp.float32)],
        in_specs=[WHOLE] * (2 * count + 1),
        out_specs=[WHOLE] * (count + 1),
        scratch_shapes=buffers(fsdp_count)
        + buffers(fsdp_count)
        + buffers(fsdp_count - 1)
        + buffers(fsdp_count - 1)
        + buffers()
        + buffers()
        + [
            pltpu.VMEM((hops, *small.shape), jnp.float32),
            pltpu.VMEM((hops, *small.shape), jnp.float32),
            dma((count, fsdp_count)),
            dma((count, fsdp_count)),
            dma((count, fsdp_count)),
            dma((count, fsdp_count)),
            dma((count,)),
            dma((count,)),
            dma((hops,)),
            dma((hops,)),
        ],
        compiler_params=pltpu.CompilerParams(collective_id=1, has_side_effects=True),
        name="scatter_gradients",
    )(*lefts, *rights, small)
    return result[:count], result[count].reshape(-1)[:length]


CHUNKS = 4


def sum_kernel(count, *refs):
    parts, outs = refs[:count], refs[count : 2 * count]
    core_in, pair_out, chip_in = (refs[(2 + i) * count : (3 + i) * count] for i in range(3))
    core_send, core_recv, chip_send, chip_recv, last_send, last_recv = refs[5 * count :]
    index = lax.axis_index("tensor")
    core = lax.rem(index, 2)
    twin = {"tensor": jnp.bitwise_xor(index, 1)}
    chip = {"tensor": jnp.bitwise_xor(index, 2)}
    greet([twin, chip])
    half = parts[0].shape[0] // 2
    rows = half // CHUNKS
    pieces = [(a, c) for a in range(count) for c in range(CHUNKS)]

    def span(side, c):
        return pl.ds(pl.multiple_of(side * half + c * rows, rows), rows)

    first, second, third = [], [], []
    for a, c in pieces:
        copy = remote(
            parts[a].at[span(1 - core, c)],
            core_in[a].at[c],
            core_send.at[a, c],
            core_recv.at[a, c],
            twin,
        )
        copy.start()
        first.append(copy)
    for (a, c), arrival in zip(pieces, first):
        arrival.wait_recv()
        pair_out[a][c] = (
            parts[a][span(core, c), :].astype(jnp.float32) + core_in[a][c].astype(jnp.float32)
        ).astype(jnp.bfloat16)
        copy = remote(
            pair_out[a].at[c], chip_in[a].at[c], chip_send.at[a, c], chip_recv.at[a, c], chip
        )
        copy.start()
        second.append(copy)
    for (a, c), arrival in zip(pieces, second):
        arrival.wait_recv()
        outs[a][span(core, c), :] = (
            pair_out[a][c].astype(jnp.float32) + chip_in[a][c].astype(jnp.float32)
        ).astype(jnp.bfloat16)
        block = outs[a].at[span(core, c)]
        copy = remote(block, block, last_send.at[a, c], last_recv.at[a, c], twin)
        copy.start()
        third.append(copy)
    for a, c in pieces:
        block = outs[a].at[span(1 - core, c)]
        remote(block, block, last_send.at[a, c], last_recv.at[a, c], twin).wait_recv()
    for copy in first + second + third:
        copy.wait_send()


def sum_tensor(parts, tensor_count, number):
    parts = [part.astype(jnp.bfloat16) for part in parts]
    if tensor_count != 4:
        return [lax.psum(part, "tensor").astype(jnp.float32) for part in parts]
    count = len(parts)
    tokens, width = parts[0].shape
    blocks = [pltpu.VMEM((CHUNKS, tokens // 2 // CHUNKS, width), jnp.bfloat16)] * (3 * count)
    totals = pl.pallas_call(
        functools.partial(sum_kernel, count),
        out_shape=[jax.ShapeDtypeStruct((tokens, width), jnp.bfloat16)] * count,
        in_specs=[WHOLE] * count,
        out_specs=[WHOLE] * count,
        scratch_shapes=blocks + [pltpu.SemaphoreType.DMA((count, CHUNKS))] * 6,
        compiler_params=pltpu.CompilerParams(collective_id=number, has_side_effects=True),
        name="sum_tensor_%d" % number,
    )(*parts)
    return [total.astype(jnp.float32) for total in totals]


def split_heads(rows):
    return rows.reshape(rows.shape[0], -1, HD).transpose(1, 0, 2)


def join_heads(heads):
    return heads.transpose(1, 0, 2).reshape(heads.shape[1], -1)


def local(
    fsdp_count,
    context_count,
    tensor_count,
    inputs,
    block_len,
    leading_norm_gain,
    leading_norm_bias,
    qkv_weight,
    qv_bias,
    out_weight,
    out_bias,
    middle_norm_gain,
    middle_norm_bias,
    up_weight,
    up_bias,
    down_weight,
    down_bias,
    cotangent,
):
    incoming_rows = inputs[0]
    block_rows = incoming_rows.shape[0]
    lengths = block_len[0]
    score_scale = 1.0 / math.sqrt(HD)
    position = lax.axis_index("context")
    slots = jnp.arange(block_rows, dtype=jnp.int32)

    def length_of(owner):
        table = jnp.arange(context_count, dtype=jnp.int32)
        return jnp.sum(jnp.where(table == owner, lengths, 0))

    live = (slots < length_of(position)).astype(jnp.float32)[:, None]
    local_width = qkv_weight.shape[2]
    qkv_full, out_full, up_full, down_full = gather_weights(
        [
            qkv_weight.reshape(qkv_weight.shape[0], 3 * local_width),
            out_weight,
            up_weight,
            down_weight,
        ],
        fsdp_count,
        context_count,
    )

    first_normed, first_normalized, first_inverse_deviation = layer_norm_forward(
        incoming_rows, leading_norm_gain, leading_norm_bias
    )
    norm1_b = first_normed.astype(jnp.bfloat16)
    projected = jnp.dot(norm1_b, qkv_full, preferred_element_type=jnp.float32)
    queries = (projected[:, :local_width] + qv_bias[0]).astype(jnp.bfloat16)
    keys = projected[:, local_width : 2 * local_width].astype(jnp.bfloat16)
    values = (projected[:, 2 * local_width :] + qv_bias[1]).astype(jnp.bfloat16)
    keys_values = jnp.concatenate([keys, values], axis=1)
    pieces = [keys_values] + [
        rotate(keys_values, "context", context_count, turn) for turn in range(1, context_count)
    ]
    owners = [(position - turn) % context_count for turn in range(context_count)]
    live_keys = jnp.concatenate([slots < length_of(owner) for owner in owners])[None, None, :]
    query_heads = split_heads(queries)
    key_heads = jnp.concatenate([split_heads(p[:, :local_width]) for p in pieces], axis=1)
    value_heads = jnp.concatenate([split_heads(p[:, local_width:]) for p in pieces], axis=1)
    scores = (
        jnp.einsum("hqe,hke->hqk", query_heads, key_heads, preferred_element_type=jnp.float32)
        * score_scale
    )
    scores = jnp.where(live_keys, scores, NEG_BIG)
    peak = jnp.max(scores, axis=2, keepdims=True)
    weights = jnp.where(live_keys, jnp.exp(scores - peak), 0.0)
    total = jnp.sum(weights, axis=2, keepdims=True)
    attn_heads = (
        jnp.einsum(
            "hqk,hke->hqe",
            weights.astype(jnp.bfloat16),
            value_heads,
            preferred_element_type=jnp.float32,
        )
        / total
    )
    attn_b = join_heads(attn_heads.astype(jnp.bfloat16))
    attn_part = jnp.dot(attn_b, out_full.T, preferred_element_type=jnp.float32)
    residual_rows = incoming_rows + sum_tensor([attn_part], tensor_count, 2)[0] + out_bias
    second_normed, second_normalized, second_inverse_deviation = layer_norm_forward(
        residual_rows, middle_norm_gain, middle_norm_bias
    )
    norm2_b = second_normed.astype(jnp.bfloat16)
    pre_act = jnp.dot(norm2_b, up_full, preferred_element_type=jnp.float32) + up_bias
    hidden = gelu_value(pre_act).astype(jnp.bfloat16)
    result_gradient = live * cotangent[0]
    grad_y_b = result_gradient.astype(jnp.bfloat16)
    hidden_gradient = jnp.dot(grad_y_b, down_full, preferred_element_type=jnp.float32) * gelu_slope(
        pre_act
    )
    grad_u_b = hidden_gradient.astype(jnp.bfloat16)
    mlp_part = jnp.dot(hidden, down_full.T, preferred_element_type=jnp.float32)
    second_norm_part = jnp.dot(grad_u_b, up_full.T, preferred_element_type=jnp.float32)
    second_norm_gradient, mlp_rows = sum_tensor([second_norm_part, mlp_part], tensor_count, 3)
    result = live * (residual_rows + mlp_rows + down_bias)
    residual_gradient = result_gradient + layer_norm_backward(
        second_norm_gradient, second_normalized, second_inverse_deviation, middle_norm_gain
    )
    grad_resid_b = residual_gradient.astype(jnp.bfloat16)
    grad_attn = jnp.dot(grad_resid_b, out_full, preferred_element_type=jnp.float32).astype(
        jnp.bfloat16
    )
    grad_attn_heads = split_heads(grad_attn)
    delta = jnp.sum(grad_attn_heads.astype(jnp.float32) * attn_heads, axis=2, keepdims=True)
    probs = weights / total
    grad_probs = jnp.einsum(
        "hqe,hke->hqk", grad_attn_heads, value_heads, preferred_element_type=jnp.float32
    )
    grad_scores = (probs * (grad_probs - delta)).astype(jnp.bfloat16)
    grad_value_heads = jnp.einsum(
        "hqk,hqe->hke",
        probs.astype(jnp.bfloat16),
        grad_attn_heads,
        preferred_element_type=jnp.float32,
    )
    grad_key_heads = score_scale * jnp.einsum(
        "hqk,hqe->hke", grad_scores, query_heads, preferred_element_type=jnp.float32
    )
    grad_query_heads = score_scale * jnp.einsum(
        "hqk,hke->hqe", grad_scores, key_heads, preferred_element_type=jnp.float32
    )
    queries_gradient = join_heads(grad_query_heads)

    def terms(turn):
        rows = slice(turn * block_rows, (turn + 1) * block_rows)
        return jnp.concatenate(
            [join_heads(grad_key_heads[:, rows]), join_heads(grad_value_heads[:, rows])], axis=1
        )

    keys_values_gradient = terms(0)
    for turn in range(1, context_count):
        keys_values_gradient = keys_values_gradient + rotate(
            terms(turn).astype(jnp.bfloat16), "context", context_count, -turn
        ).astype(jnp.float32)
    grad_p = jnp.concatenate([queries_gradient, keys_values_gradient], axis=1).astype(jnp.bfloat16)
    first_norm_gradient = sum_tensor(
        [jnp.dot(grad_p, qkv_full.T, preferred_element_type=jnp.float32)], tensor_count, 4
    )[0]
    input_gradient = residual_gradient + layer_norm_backward(
        first_norm_gradient, first_normalized, first_inverse_deviation, leading_norm_gain
    )
    small = jnp.concatenate(
        [
            jnp.sum(residual_gradient, axis=0),
            jnp.sum(second_norm_gradient * second_normalized, axis=0),
            jnp.sum(second_norm_gradient, axis=0),
            jnp.sum(result_gradient, axis=0),
            jnp.sum(first_norm_gradient * first_normalized, axis=0),
            jnp.sum(first_norm_gradient, axis=0),
            jnp.sum(queries_gradient, axis=0),
            jnp.sum(keys_values_gradient[:, local_width:], axis=0),
            jnp.sum(hidden_gradient, axis=0),
        ]
    )
    (down_owned, up_owned, out_owned, qkv_owned), small = scatter_gradients(
        [(grad_y_b, hidden), (norm2_b, grad_u_b), (grad_resid_b, attn_b), (norm1_b, grad_p)],
        small,
        fsdp_count,
        context_count,
    )
    width = incoming_rows.shape[1]
    return (
        result[None],
        input_gradient[None],
        small[4 * width : 5 * width],
        small[5 * width : 6 * width],
        qkv_owned.reshape(qkv_weight.shape),
        small[6 * width : 6 * width + 2 * local_width].reshape(2, local_width),
        out_owned,
        small[:width],
        small[width : 2 * width],
        small[2 * width : 3 * width],
        up_owned,
        small[6 * width + 2 * local_width :],
        down_owned,
        small[3 * width : 4 * width],
    )


def solution(mesh):
    in_specs = (
        P("fsdp", "context", None),
        P("fsdp", None),
        P(),
        P(),
        P("fsdp", None, "tensor"),
        P(None, "tensor"),
        P("fsdp", "tensor"),
        P(),
        P(),
        P(),
        P("fsdp", "tensor"),
        P("tensor"),
        P("fsdp", "tensor"),
        P(),
        P("fsdp", "context", None),
    )
    out_specs = (
        P("fsdp", "context", None),
        P("fsdp", "context", None),
        P(),
        P(),
        P("fsdp", None, "tensor"),
        P(None, "tensor"),
        P("fsdp", "tensor"),
        P(),
        P(),
        P(),
        P("fsdp", "tensor"),
        P("tensor"),
        P("fsdp", "tensor"),
        P(),
    )
    return jax.shard_map(functools.partial(local, mesh.shape["fsdp"], mesh.shape["context"], mesh.shape["tensor"]), mesh=mesh, in_specs=in_specs, out_specs=out_specs, check_vma=False)
```

```python
import functools
import math

import jax
import jax.numpy as jnp
from jax import lax
from jax.experimental import pallas as pl
from jax.experimental.pallas import tpu as pltpu
from jax.sharding import PartitionSpec as P

HD = 64


EPS = 1e-06
SQRT_HALF = 0.7071067811865476
INV_ROOT_TAU = 0.3989422804014327
NEG_BIG = -1e30


def layer_norm_forward(rows, norm_gain, norm_bias):
    centered_rows = rows - jnp.mean(rows, axis=-1, keepdims=True)
    inverse_deviation = lax.rsqrt(
        jnp.mean(centered_rows * centered_rows, axis=-1, keepdims=True) + EPS
    )
    normalized_rows = centered_rows * inverse_deviation
    return (normalized_rows * norm_gain + norm_bias, normalized_rows, inverse_deviation)


def layer_norm_backward(output_gradient, normalized_rows, inverse_deviation, norm_gain):
    scaled_rows = output_gradient * norm_gain
    return inverse_deviation * (
        scaled_rows
        - jnp.mean(scaled_rows, axis=-1, keepdims=True)
        - normalized_rows * jnp.mean(scaled_rows * normalized_rows, axis=-1, keepdims=True)
    )


def gelu_value(value):
    return 0.5 * value * (1.0 + lax.erf(value * SQRT_HALF))


def gelu_slope(value):
    return 0.5 * (1.0 + lax.erf(value * SQRT_HALF)) + value * INV_ROOT_TAU * jnp.exp(
        -0.5 * value * value
    )


def rotate(x, axis, count, step):
    return lax.ppermute(x, axis, [(i, (i + step) % count) for i in range(count)])


MESH = pl.DeviceIdType.MESH
WHOLE = pl.BlockSpec(memory_space=pltpu.VMEM)


def remote(source, target, send, receive, where):
    copy = pltpu.make_async_remote_copy(
        src_ref=source,
        dst_ref=target,
        send_sem=send,
        recv_sem=receive,
        device_id=where,
        device_id_type=MESH,
    )
    return copy


def rows_of(index, rows):
    return pl.ds(pl.multiple_of(index * rows, rows), rows)


def greet(partners):
    barrier = pltpu.get_barrier_semaphore()
    for partner in partners:
        pl.semaphore_signal(barrier, inc=1, device_id=partner, device_id_type=MESH)
    pl.semaphore_wait(barrier, len(partners))


def gather_kernel(count, fsdp_count, *refs):
    shards, fulls = refs[:count], refs[count : 2 * count]
    up_send, down_send, line_recv, side_send, side_recv = refs[2 * count :]
    place, position = lax.axis_index("fsdp"), lax.axis_index("context")
    mate = {"context": 1 - position}
    above, below = {"fsdp": place + 1}, {"fsdp": place - 1}
    has_above, has_below = place < fsdp_count - 1, place > 0
    greet(
        [mate] + [{"fsdp": lax.rem(place + step, fsdp_count)} for step in range(1, fsdp_count)]
    )

    def part(w, owner):
        shard_rows = shards[w].shape[0]
        half = shard_rows // 2
        start = pl.multiple_of(owner * shard_rows + position * half, half)
        return fulls[w].at[pl.ds(start, half)]

    def far_part(w, owner):
        shard_rows = shards[w].shape[0]
        half = shard_rows // 2
        start = pl.multiple_of(owner * shard_rows + (1 - position) * half, half)
        return fulls[w].at[pl.ds(start, half)]

    def own(w):
        return shards[w].at[rows_of(position, shards[w].shape[0] // 2)]

    def upward(w, owner, source):
        return remote(source, part(w, owner), up_send.at[w, owner], line_recv.at[w, owner], above)

    def downward(w, owner, source):
        return remote(
            source, part(w, owner), down_send.at[w, owner], line_recv.at[w, owner], below
        )

    def sideways(w, owner):
        block = part(w, owner)
        return remote(block, block, side_send.at[w, owner], side_recv.at[w, owner], mate)

    for w in range(count):

        @pl.when(has_above)
        def _():
            upward(w, place, own(w)).start()

        @pl.when(has_below)
        def _():
            downward(w, place, own(w)).start()

    for w in range(count):
        fulls[w][rows_of(place, shards[w].shape[0]), :] = shards[w][...]
    for distance in range(1, fsdp_count):
        for w in range(count):
            low, high = place - distance, place + distance

            @pl.when(low >= 0)
            def _():
                block = part(w, low)
                upward(w, low, block).wait_recv()

                @pl.when(has_above)
                def _():
                    upward(w, low, block).start()

                sideways(w, low).start()

            @pl.when(high < fsdp_count)
            def _():
                block = part(w, high)
                downward(w, high, block).wait_recv()

                @pl.when(has_below)
                def _():
                    downward(w, high, block).start()

                sideways(w, high).start()

    for w in range(count):

        @pl.when(has_above)
        def _():
            upward(w, place, own(w)).wait_send()

        @pl.when(has_below)
        def _():
            downward(w, place, own(w)).wait_send()

        for distance in range(1, fsdp_count):
            low, high = place - distance, place + distance

            @pl.when(low >= 0)
            def _():
                block = part(w, low)

                @pl.when(has_above)
                def _():
                    upward(w, low, block).wait_send()

                sideways(w, low).wait_send()
                other = far_part(w, low)
                remote(
                    other, other, side_send.at[w, low], side_recv.at[w, low], mate
                ).wait_recv()

            @pl.when(high < fsdp_count)
            def _():
                block = part(w, high)

                @pl.when(has_below)
                def _():
                    downward(w, high, block).wait_send()

                sideways(w, high).wait_send()
                other = far_part(w, high)
                remote(
                    other, other, side_send.at[w, high], side_recv.at[w, high], mate
                ).wait_recv()


def gather_weights(shards, fsdp_count, context_count):
    if not direct(fsdp_count, context_count):
        return [lax.all_gather(shard, "fsdp", axis=0, tiled=True) for shard in shards]
    count = len(shards)
    sems = pltpu.SemaphoreType.DMA((count, fsdp_count))
    return pl.pallas_call(
        functools.partial(gather_kernel, count, fsdp_count),
        out_shape=[
            jax.ShapeDtypeStruct((fsdp_count * x.shape[0], x.shape[1]), x.dtype) for x in shards
        ],
        in_specs=[WHOLE] * count,
        out_specs=[WHOLE] * count,
        scratch_shapes=[sems] * 5,
        compiler_params=pltpu.CompilerParams(collective_id=0, has_side_effects=True),
        name="gather_weights",
    )(*shards)


def direct(fsdp_count, context_count):
    return context_count == 2 and fsdp_count in (2, 4)


def scatter_kernel(count, fsdp_count, *refs):
    lefts, rights = refs[:count], refs[count : 2 * count]
    small, owned = refs[2 * count : 2 * count + 2]
    outs = refs[2 * count + 2 : 3 * count + 2]
    small_out, owned_out = refs[3 * count + 2 : 3 * count + 4]
    rest = refs[3 * count + 4 :]
    side_out, side_in, line_out, line_in, last_out, last_in = (
        rest[i * count : (i + 1) * count] for i in range(6)
    )
    (
        small_sum,
        small_in,
        side_send,
        side_recv,
        line_send,
        line_recv,
        last_send,
        last_recv,
        small_send,
        small_recv,
        owned_in,
        owned_sems,
    ) = rest[6 * count :]
    place, position = lax.axis_index("fsdp"), lax.axis_index("context")
    other = 1 - position
    mate = {"context": other}
    features = lefts[0].shape[1]
    shard_rows = features // fsdp_count
    half = shard_rows // 2
    greet(
        [mate] + [{"fsdp": lax.rem(place + step, fsdp_count)} for step in range(1, fsdp_count)]
    )

    def product(w, step, side):
        owner = lax.rem(place + step, fsdp_count)
        start = pl.multiple_of(owner * shard_rows + side * half, half)
        return lax.dot_general(
            lefts[w][:, pl.ds(start, half)],
            rights[w][...],
            (((0,), (0,)), ((), ())),
            preferred_element_type=jnp.float32,
        )

    hops = [mate]
    bit = 1
    while bit < fsdp_count:
        hops.append({"fsdp": jnp.bitwise_xor(place, bit)})
        bit *= 2
    small_copies = []

    def small_hop(hop):
        source = small if hop == 0 else small_sum.at[hop - 1]
        copy = remote(
            source, small_in.at[hop], small_send.at[hop], small_recv.at[hop], hops[hop]
        )
        copy.start()
        small_copies.append(copy)

    def small_add(hop):
        small_copies[hop].wait_recv()
        before = small[...] if hop == 0 else small_sum[hop - 1]
        after = before + small_in[hop]
        if hop + 1 == len(hops):
            small_out[...] = after
        else:
            small_sum[hop] = after

    small_hop(0)
    sends = []
    side_copies = {}
    order = [step % fsdp_count for step in range(1, fsdp_count + 1)]
    for w in range(count):
        for step in order:
            side_out[w][step] = product(w, step, other).astype(jnp.bfloat16)
            copy = remote(
                side_out[w].at[step],
                side_in[w].at[step],
                side_send.at[w, step],
                side_recv.at[w, step],
                mate,
            )
            copy.start()
            side_copies[w, step] = copy
            sends.append(copy)
        if w < len(hops):
            small_add(w)
            if w + 1 < len(hops):
                small_hop(w + 1)
    for hop in range(count, len(hops)):
        small_add(hop)
        if hop + 1 < len(hops):
            small_hop(hop + 1)
    owned_copy = remote(owned, owned_in, owned_sems.at[0], owned_sems.at[1], mate)
    owned_copy.start()
    sends.append(owned_copy)
    line_copies = {}
    last_copies = []

    def settle(w):
        total = outs[w][rows_of(position, half), :]
        for step in range(1, fsdp_count):
            line_copies[w, step].wait_recv()
            total = total + line_in[w][step - 1].astype(jnp.float32)
        rounded = total.astype(jnp.bfloat16)
        last_out[w][...] = rounded
        copy = remote(last_out[w], last_in[w], last_send.at[w], last_recv.at[w], mate)
        copy.start()
        last_copies.append(copy)
        sends.append(copy)
        outs[w][rows_of(position, half), :] = rounded.astype(jnp.float32)

    for w in range(count):
        for step in order:
            mine = product(w, step, position)
            side_copies[w, step].wait_recv()
            mine = mine + side_in[w][step].astype(jnp.float32)
            if step == 0:
                outs[w][rows_of(position, half), :] = mine
                continue
            line_out[w][step - 1] = mine.astype(jnp.bfloat16)
            copy = remote(
                line_out[w].at[step - 1],
                line_in[w].at[step - 1],
                line_send.at[w, step - 1],
                line_recv.at[w, step - 1],
                {"fsdp": lax.rem(place + step, fsdp_count)},
            )
            copy.start()
            line_copies[w, step] = copy
            sends.append(copy)
        if w > 0:
            settle(w - 1)
    settle(count - 1)
    owned_copy.wait_recv()
    owned_out[...] = owned[...].astype(jnp.float32) + owned_in[...].astype(jnp.float32)
    for w in range(count):
        last_copies[w].wait_recv()
        outs[w][rows_of(other, half), :] = last_in[w][...].astype(jnp.float32)
    for copy in small_copies + sends:
        copy.wait_send()


def scatter_plain(left, right):
    whole = jnp.dot(left.T, right, preferred_element_type=jnp.float32)
    return lax.psum_scatter(whole.astype(jnp.bfloat16), "fsdp", scatter_dimension=0, tiled=True)


def scatter_gradients(pairs, small, owned, fsdp_count, context_count):
    if not direct(fsdp_count, context_count):
        parts = [scatter_plain(*pair) for pair in pairs] + [owned]
        sums = [lax.psum(part, "context").astype(jnp.float32) for part in parts]
        return sums, lax.psum(small, ("fsdp", "context"))
    count = len(pairs)
    lefts, rights = [p[0] for p in pairs], [p[1] for p in pairs]
    length = small.shape[0]
    padded = -(-length // 1024) * 1024
    small = jnp.pad(small, (0, padded - length)).reshape(padded // 128, 128)
    shard_rows = lefts[0].shape[1] // fsdp_count
    half = shard_rows // 2
    widths = [x.shape[1] for x in rights]

    def buffers(*lead):
        return [pltpu.VMEM((*lead, half, width), jnp.bfloat16) for width in widths]

    hops = 1 + (fsdp_count - 1).bit_length()
    dma = pltpu.SemaphoreType.DMA
    result = pl.pallas_call(
        functools.partial(scatter_kernel, count, fsdp_count),
        out_shape=[jax.ShapeDtypeStruct((shard_rows, width), jnp.float32) for width in widths]
        + [
            jax.ShapeDtypeStruct(small.shape, jnp.float32),
            jax.ShapeDtypeStruct(owned.shape, jnp.float32),
        ],
        in_specs=[WHOLE] * (2 * count + 2),
        out_specs=[WHOLE] * (count + 2),
        scratch_shapes=buffers(fsdp_count)
        + buffers(fsdp_count)
        + buffers(fsdp_count - 1)
        + buffers(fsdp_count - 1)
        + buffers()
        + buffers()
        + [
            pltpu.VMEM((hops, *small.shape), jnp.float32),
            pltpu.VMEM((hops, *small.shape), jnp.float32),
            dma((count, fsdp_count)),
            dma((count, fsdp_count)),
            dma((count, fsdp_count)),
            dma((count, fsdp_count)),
            dma((count,)),
            dma((count,)),
            dma((hops,)),
            dma((hops,)),
            pltpu.VMEM(owned.shape, owned.dtype),
            dma((2,)),
        ],
        compiler_params=pltpu.CompilerParams(collective_id=1, has_side_effects=True),
        name="scatter_gradients",
    )(*lefts, *rights, small, owned)
    return result[:count] + result[count + 1 :], result[count].reshape(-1)[:length]


CHUNKS = 4


def sum_kernel(count, *refs):
    parts, outs = refs[:count], refs[count : 2 * count]
    core_in, pair_out, chip_in = (refs[(2 + i) * count : (3 + i) * count] for i in range(3))
    core_send, core_recv, chip_send, chip_recv, last_send, last_recv = refs[5 * count :]
    index = lax.axis_index("tensor")
    core = lax.rem(index, 2)
    twin = {"tensor": jnp.bitwise_xor(index, 1)}
    chip = {"tensor": jnp.bitwise_xor(index, 2)}
    greet([twin, chip])
    half = parts[0].shape[0] // 2
    rows = half // CHUNKS
    pieces = [(a, c) for a in range(count) for c in range(CHUNKS)]

    def span(side, c):
        return pl.ds(pl.multiple_of(side * half + c * rows, rows), rows)

    first, second, third = [], [], []
    for a, c in pieces:
        copy = remote(
            parts[a].at[span(1 - core, c)],
            core_in[a].at[c],
            core_send.at[a, c],
            core_recv.at[a, c],
            twin,
        )
        copy.start()
        first.append(copy)
    for (a, c), arrival in zip(pieces, first):
        arrival.wait_recv()
        pair_out[a][c] = (
            parts[a][span(core, c), :].astype(jnp.float32) + core_in[a][c].astype(jnp.float32)
        ).astype(jnp.bfloat16)
        copy = remote(
            pair_out[a].at[c], chip_in[a].at[c], chip_send.at[a, c], chip_recv.at[a, c], chip
        )
        copy.start()
        second.append(copy)
    for (a, c), arrival in zip(pieces, second):
        arrival.wait_recv()
        outs[a][span(core, c), :] = (
            pair_out[a][c].astype(jnp.float32) + chip_in[a][c].astype(jnp.float32)
        ).astype(jnp.bfloat16)
        block = outs[a].at[span(core, c)]
        copy = remote(block, block, last_send.at[a, c], last_recv.at[a, c], twin)
        copy.start()
        third.append(copy)
    for a, c in pieces:
        block = outs[a].at[span(1 - core, c)]
        remote(block, block, last_send.at[a, c], last_recv.at[a, c], twin).wait_recv()
    for copy in first + second + third:
        copy.wait_send()


def sum_tensor(parts, tensor_count, number):
    parts = [part.astype(jnp.bfloat16) for part in parts]
    if tensor_count != 4:
        return [lax.psum(part, "tensor").astype(jnp.float32) for part in parts]
    count = len(parts)
    tokens, width = parts[0].shape
    blocks = [pltpu.VMEM((CHUNKS, tokens // 2 // CHUNKS, width), jnp.bfloat16)] * (3 * count)
    totals = pl.pallas_call(
        functools.partial(sum_kernel, count),
        out_shape=[jax.ShapeDtypeStruct((tokens, width), jnp.bfloat16)] * count,
        in_specs=[WHOLE] * count,
        out_specs=[WHOLE] * count,
        scratch_shapes=blocks + [pltpu.SemaphoreType.DMA((count, CHUNKS))] * 6,
        compiler_params=pltpu.CompilerParams(collective_id=number, has_side_effects=True),
        name="sum_tensor_%d" % number,
    )(*parts)
    return [total.astype(jnp.float32) for total in totals]


def split_heads(rows):
    return rows.reshape(rows.shape[0], -1, HD).transpose(1, 0, 2)


def join_heads(heads):
    return heads.transpose(1, 0, 2).reshape(heads.shape[1], -1)


def local(
    fsdp_count,
    context_count,
    tensor_count,
    inputs,
    block_len,
    leading_norm_gain,
    leading_norm_bias,
    qkv_weight,
    qv_bias,
    out_weight,
    out_bias,
    middle_norm_gain,
    middle_norm_bias,
    up_weight,
    up_bias,
    down_weight,
    down_bias,
    cotangent,
):
    incoming_rows = inputs[0]
    block_rows = incoming_rows.shape[0]
    lengths = block_len[0]
    score_scale = 1.0 / math.sqrt(HD)
    position = lax.axis_index("context")
    slots = jnp.arange(block_rows, dtype=jnp.int32)

    def length_of(owner):
        table = jnp.arange(context_count, dtype=jnp.int32)
        return jnp.sum(jnp.where(table == owner, lengths, 0))

    live = (slots < length_of(position)).astype(jnp.float32)[:, None]
    local_width = qkv_weight.shape[2]
    qkv_full, out_full, up_full, down_full = gather_weights(
        [
            qkv_weight.reshape(qkv_weight.shape[0], 3 * local_width),
            out_weight,
            up_weight,
            down_weight,
        ],
        fsdp_count,
        context_count,
    )

    first_normed, first_normalized, first_inverse_deviation = layer_norm_forward(
        incoming_rows, leading_norm_gain, leading_norm_bias
    )
    norm1_b = first_normed.astype(jnp.bfloat16)
    projected = jnp.dot(norm1_b, qkv_full, preferred_element_type=jnp.float32)
    queries = (projected[:, :local_width] + qv_bias[0]).astype(jnp.bfloat16)
    keys = projected[:, local_width : 2 * local_width].astype(jnp.bfloat16)
    values = (projected[:, 2 * local_width :] + qv_bias[1]).astype(jnp.bfloat16)
    keys_values = jnp.concatenate([keys, values], axis=1)
    pieces = [keys_values] + [
        rotate(keys_values, "context", context_count, turn) for turn in range(1, context_count)
    ]
    owners = [(position - turn) % context_count for turn in range(context_count)]
    live_keys = jnp.concatenate([slots < length_of(owner) for owner in owners])[None, None, :]
    query_heads = split_heads(queries)
    key_heads = jnp.concatenate([split_heads(p[:, :local_width]) for p in pieces], axis=1)
    value_heads = jnp.concatenate([split_heads(p[:, local_width:]) for p in pieces], axis=1)
    scores = (
        jnp.einsum("hqe,hke->hqk", query_heads, key_heads, preferred_element_type=jnp.float32)
        * score_scale
    )
    scores = jnp.where(live_keys, scores, NEG_BIG)
    peak = jnp.max(scores, axis=2, keepdims=True)
    weights = jnp.where(live_keys, jnp.exp(scores - peak), 0.0)
    total = jnp.sum(weights, axis=2, keepdims=True)
    attn_heads = (
        jnp.einsum(
            "hqk,hke->hqe",
            weights.astype(jnp.bfloat16),
            value_heads,
            preferred_element_type=jnp.float32,
        )
        / total
    )
    attn_b = join_heads(attn_heads.astype(jnp.bfloat16))
    attn_part = jnp.dot(attn_b, out_full.T, preferred_element_type=jnp.float32)
    residual_rows = incoming_rows + sum_tensor([attn_part], tensor_count, 2)[0] + out_bias
    second_normed, second_normalized, second_inverse_deviation = layer_norm_forward(
        residual_rows, middle_norm_gain, middle_norm_bias
    )
    norm2_b = second_normed.astype(jnp.bfloat16)
    pre_act = jnp.dot(norm2_b, up_full, preferred_element_type=jnp.float32) + up_bias
    hidden = gelu_value(pre_act).astype(jnp.bfloat16)
    result_gradient = live * cotangent[0]
    grad_y_b = result_gradient.astype(jnp.bfloat16)
    down_part = scatter_plain(grad_y_b, hidden)
    hidden_gradient = jnp.dot(grad_y_b, down_full, preferred_element_type=jnp.float32) * gelu_slope(
        pre_act
    )
    grad_u_b = hidden_gradient.astype(jnp.bfloat16)
    mlp_part = jnp.dot(hidden, down_full.T, preferred_element_type=jnp.float32)
    second_norm_part = jnp.dot(grad_u_b, up_full.T, preferred_element_type=jnp.float32)
    second_norm_gradient, mlp_rows = sum_tensor([second_norm_part, mlp_part], tensor_count, 3)
    result = live * (residual_rows + mlp_rows + down_bias)
    residual_gradient = result_gradient + layer_norm_backward(
        second_norm_gradient, second_normalized, second_inverse_deviation, middle_norm_gain
    )
    grad_resid_b = residual_gradient.astype(jnp.bfloat16)
    grad_attn = jnp.dot(grad_resid_b, out_full, preferred_element_type=jnp.float32).astype(
        jnp.bfloat16
    )
    grad_attn_heads = split_heads(grad_attn)
    delta = jnp.sum(grad_attn_heads.astype(jnp.float32) * attn_heads, axis=2, keepdims=True)
    probs = weights / total
    grad_probs = jnp.einsum(
        "hqe,hke->hqk", grad_attn_heads, value_heads, preferred_element_type=jnp.float32
    )
    grad_scores = (probs * (grad_probs - delta)).astype(jnp.bfloat16)
    grad_value_heads = jnp.einsum(
        "hqk,hqe->hke",
        probs.astype(jnp.bfloat16),
        grad_attn_heads,
        preferred_element_type=jnp.float32,
    )
    grad_key_heads = score_scale * jnp.einsum(
        "hqk,hqe->hke", grad_scores, query_heads, preferred_element_type=jnp.float32
    )
    grad_query_heads = score_scale * jnp.einsum(
        "hqk,hke->hqe", grad_scores, key_heads, preferred_element_type=jnp.float32
    )
    queries_gradient = join_heads(grad_query_heads)

    def terms(turn):
        rows = slice(turn * block_rows, (turn + 1) * block_rows)
        return jnp.concatenate(
            [join_heads(grad_key_heads[:, rows]), join_heads(grad_value_heads[:, rows])], axis=1
        )

    keys_values_gradient = terms(0)
    for turn in range(1, context_count):
        keys_values_gradient = keys_values_gradient + rotate(
            terms(turn).astype(jnp.bfloat16), "context", context_count, -turn
        ).astype(jnp.float32)
    grad_p = jnp.concatenate([queries_gradient, keys_values_gradient], axis=1).astype(jnp.bfloat16)
    first_norm_gradient = sum_tensor(
        [jnp.dot(grad_p, qkv_full.T, preferred_element_type=jnp.float32)], tensor_count, 4
    )[0]
    input_gradient = residual_gradient + layer_norm_backward(
        first_norm_gradient, first_normalized, first_inverse_deviation, leading_norm_gain
    )
    small = jnp.concatenate(
        [
            jnp.sum(residual_gradient, axis=0),
            jnp.sum(second_norm_gradient * second_normalized, axis=0),
            jnp.sum(second_norm_gradient, axis=0),
            jnp.sum(result_gradient, axis=0),
            jnp.sum(first_norm_gradient * first_normalized, axis=0),
            jnp.sum(first_norm_gradient, axis=0),
            jnp.sum(queries_gradient, axis=0),
            jnp.sum(keys_values_gradient[:, local_width:], axis=0),
            jnp.sum(hidden_gradient, axis=0),
        ]
    )
    (up_owned, out_owned, qkv_owned, down_owned), small = scatter_gradients(
        [(norm2_b, grad_u_b), (grad_resid_b, attn_b), (norm1_b, grad_p)],
        small,
        down_part,
        fsdp_count,
        context_count,
    )
    width = incoming_rows.shape[1]
    return (
        result[None],
        input_gradient[None],
        small[4 * width : 5 * width],
        small[5 * width : 6 * width],
        qkv_owned.reshape(qkv_weight.shape),
        small[6 * width : 6 * width + 2 * local_width].reshape(2, local_width),
        out_owned,
        small[:width],
        small[width : 2 * width],
        small[2 * width : 3 * width],
        up_owned,
        small[6 * width + 2 * local_width :],
        down_owned,
        small[3 * width : 4 * width],
    )


def solution(mesh):
    in_specs = (
        P("fsdp", "context", None),
        P("fsdp", None),
        P(),
        P(),
        P("fsdp", None, "tensor"),
        P(None, "tensor"),
        P("fsdp", "tensor"),
        P(),
        P(),
        P(),
        P("fsdp", "tensor"),
        P("tensor"),
        P("fsdp", "tensor"),
        P(),
        P("fsdp", "context", None),
    )
    out_specs = (
        P("fsdp", "context", None),
        P("fsdp", "context", None),
        P(),
        P(),
        P("fsdp", None, "tensor"),
        P(None, "tensor"),
        P("fsdp", "tensor"),
        P(),
        P(),
        P(),
        P("fsdp", "tensor"),
        P("tensor"),
        P("fsdp", "tensor"),
        P(),
    )
    return jax.shard_map(functools.partial(local, mesh.shape["fsdp"], mesh.shape["context"], mesh.shape["tensor"]), mesh=mesh, in_specs=in_specs, out_specs=out_specs, check_vma=False)
```
